32 devices in a mesh: dev: 8 (over y, x, core), rep: 4 (over z).
Axes of the slice: x: 2, y: 2, z: 4, core: 2. Of those that a mesh axis runs over, the one named last changes fastest.
Arguments:
- images: bfloat16 [64, 577, 1024], P(('dev', 'rep')), may hold values from -6 to 6
- norm1_gain: bfloat16 [1024], P(('dev', 'rep')), may hold values from 0.25 to 1.75
- norm1_bias: bfloat16 [1024], P(('dev', 'rep')), may hold values from -3 to 3
- qkv_weight: bfloat16 [1024, 3072], P(('dev', 'rep')), may hold values from -0.1875 to 0.1875
- qv_bias: bfloat16 [2048], P(('dev', 'rep')), may hold values from -1.1953125 to 1.1953125
- out_weight: bfloat16 [1024, 1024], P(('dev', 'rep')), may hold values from -0.75 to 0.75
- out_bias: bfloat16 [1024], P(('dev', 'rep')), may hold values from -3 to 3
- norm2_gain: bfloat16 [1024], P(('dev', 'rep')), may hold values from 0.25 to 1.75
- norm2_bias: bfloat16 [1024], P(('dev', 'rep')), may hold values from -3 to 3
- up_weight: bfloat16 [1024, 4096], P(('dev', 'rep')), may hold values from -0.1875 to 0.1875
- up_bias: bfloat16 [4096], P(('dev', 'rep')), may hold values from -3 to 3
- down_weight: bfloat16 [4096, 1024], P(('dev', 'rep')), may hold values from -0.125 to 0.125
- down_bias: bfloat16 [1024], P(('dev', 'rep')), may hold values from -3 to 3
- cotangent: bfloat16 [64, 577, 1024], P(('dev', 'rep')), may hold values from -6 to 6
- filled: int32 [64], P(('dev', 'rep')), may hold values 0 or 1
Outputs:
- output: bfloat16 [64, 577, 1024], P(('dev', 'rep'))
- input_grad: bfloat16 [64, 577, 1024], P(('dev', 'rep'))
- norm1_gain_grad: float32 [1024], P(('dev', 'rep'))
- norm1_bias_grad: float32 [1024], P(('dev', 'rep'))
- qkv_weight_grad: float32 [1024, 3072], P(('dev', 'rep'))
- qv_bias_grad: float32 [2048], P(('dev', 'rep'))
- out_weight_grad: float32 [1024, 1024], P(('dev', 'rep'))
- out_bias_grad: float32 [1024], P(('dev', 'rep'))
- norm2_gain_grad: float32 [1024], P(('dev', 'rep'))
- norm2_bias_grad: float32 [1024], P(('dev', 'rep'))
- up_weight_grad: float32 [1024, 4096], P(('dev', 'rep'))
- up_bias_grad: float32 [4096], P(('dev', 'rep'))
- down_weight_grad: float32 [4096, 1024], P(('dev', 'rep'))
- down_bias_grad: float32 [1024], P(('dev', 'rep'))
The draws below stay inside these ranges and needn't reach their ends.
Inputs may be any that keep to these rules, and one draw needn't show every extreme that they name: `filled`: 1 marks a slot that holds an image, 0 an empty slot.
All inputs are finite; a program needn't handle non-finite values. No bound on the sum of `filled` on one device may be relied on, other than what follows from the above.
Results may differ from the reference program's by a relative error of at most 0.012.
Values may be sent and summed in bfloat16 or wider, within the bound.
A program may use at most 320 MiB of HBM per device.

```python
import math
import jax
import jax.numpy as jnp
from jax import lax

D = 1024
HEADS = 16
HD = 64
FF = 4096
SEQ = 577
SLOTS = 64


def set_ends(array, key, least, largest):
    dims = array.shape
    spot = [jax.random.randint(jax.random.fold_in(key, axis), (), 0, dims[axis]) for axis in range(len(dims))]
    array = array.at[tuple(spot)].set(least)
    longest = dims.index(max(dims))
    spot[longest] = (spot[longest] + 1) % dims[longest]
    return array.at[tuple(spot)].set(largest)


def block_scale(own_key, dims, split, smallest, high):
    def one(axis_at, blocks):
        draws = jax.random.uniform(jax.random.fold_in(jax.random.fold_in(own_key, 6), axis_at), (blocks,), jnp.float32, smallest / len(split), high / len(split))
        return jnp.repeat(jnp.exp(draws), dims[axis_at] // blocks).reshape((-1,) + (1,) * (len(dims) - axis_at - 1))

    loudness = one(*split[0])
    for cut in split[1:]:
        loudness = loudness * one(*cut)
    return loudness


def noise(stream_key, shape, scale, most, cuts=(), held_as=jnp.bfloat16):
    drawn = jax.random.normal(stream_key, shape, jnp.float32) * scale
    if len(cuts) > 0:
        drawn = block_scale(stream_key, shape, cuts, -0.22, 0.18) * drawn
    return jnp.clip(drawn, min=-most, max=most).astype(held_as)


def setup_inputs(seed: int = 0) -> dict:
    seeds = jax.random.split(jax.random.key(seed), 16)
    return {
        "images": noise(seeds[0], (SLOTS, SEQ, D), 1.0, 6.0, ((0, 32),)),
        "norm1_gain": jnp.clip(1.0 + 0.15 * jax.random.normal(seeds[1], (D,), jnp.float32), 0.25, 1.75).astype(jnp.bfloat16),
        "norm1_bias": noise(seeds[2], (D,), 0.5, 3.0, ((0, 32),)),
        "qkv_weight": noise(seeds[3], (D, 3 * D), D ** -0.5, 0.1875, ((0, 32),)),
        "qv_bias": noise(seeds[4], (2 * D,), 0.2, 1.1953125, ((0, 32),)),
        "out_weight": noise(seeds[5], (D, D), 64 ** -0.5, 0.75, ((0, 32),)),
        "out_bias": noise(seeds[6], (D,), 0.5, 3.0, ((0, 32),)),
        "norm2_gain": jnp.clip(1.0 + 0.15 * jax.random.normal(seeds[7], (D,), jnp.float32), 0.25, 1.75).astype(jnp.bfloat16),
        "norm2_bias": noise(seeds[8], (D,), 0.5, 3.0, ((0, 32),)),
        "up_weight": noise(seeds[9], (D, FF), D ** -0.5, 0.1875, ((0, 32),)),
        "up_bias": noise(seeds[10], (FF,), 0.5, 3.0, ((0, 32),)),
        "down_weight": noise(seeds[11], (FF, D), (FF // 2) ** -0.5, 0.125, ((0, 32),)),
        "down_bias": noise(seeds[12], (D,), 0.5, 3.0, ((0, 32),)),
        "cotangent": noise(seeds[13], (SLOTS, SEQ, D), 1.0, 6.0, ((0, 32),)),
        "filled": set_ends((jax.random.randint(seeds[14], (SLOTS,), 0, 8) < 7).astype(jnp.int32), jax.random.fold_in(seeds[14], 1), 0, 1),
    }


@jax.custom_vjp
def low(v):
    return lax.optimization_barrier(v.astype(jnp.bfloat16)).astype(jnp.float32)

@jax.custom_vjp
def low_back(v):
    return v

def low_keep(v):
    return (low(v), None)

def low_pass(kept, grad):
    return (grad,)

def back_keep(v):
    return (v, None)

def back_low(kept, grad):
    return (low(grad),)
low.defvjp(low_keep, low_pass)
low_back.defvjp(back_keep, back_low)

def layer_norm(values, gain, shift):
    centred = values - lax.optimization_barrier(jnp.mean(values, axis=-1, keepdims=True))
    spread = lax.optimization_barrier(jnp.mean(centred * centred, axis=-1, keepdims=True))
    return centred * lax.rsqrt(spread + 1e-06) * gain + shift

def product(left, right):
    return jnp.dot(left, right, precision=lax.Precision.HIGHEST, preferred_element_type=jnp.float32)

def forward(params, image):
    norm1_gain, norm1_bias, qkv_weight, qv_bias, out_weight, out_bias, norm2_gain, norm2_bias, up_weight, up_bias, down_weight, down_bias = params
    width = image.shape[1]
    scale = 1.0 / math.sqrt(HD)
    normed_one = low(layer_norm(image, norm1_gain, norm1_bias))
    bias_full = jnp.concatenate([qv_bias[:width], jnp.zeros((width,), jnp.float32), qv_bias[width:]])
    joined = low_back(low(product(normed_one, qkv_weight) + bias_full))
    parts = joined.reshape(SEQ, 3, HEADS, HD)
    queries = parts[:, 0]
    keys = parts[:, 1]
    values = parts[:, 2]
    scores = low_back(jnp.einsum('qhd,khd->hqk', queries, keys, precision=lax.Precision.HIGHEST) * scale)
    probs = low(jax.nn.softmax(scores, axis=-1))
    mixed = jnp.einsum('hqk,khd->qhd', probs, values, precision=lax.Precision.HIGHEST)
    heads_out = low_back(low(mixed.reshape(SEQ, width)))
    attn = low_back(product(heads_out, out_weight) + out_bias)
    middle = image + attn
    normed_two = low(layer_norm(middle, norm2_gain, norm2_bias))
    hidden_pre = low_back(product(normed_two, up_weight) + up_bias)
    activated = low(jax.nn.gelu(hidden_pre, approximate=False))
    branch = low_back(product(activated, down_weight) + down_bias)
    return middle + branch

def reference(images, norm1_gain, norm1_bias, qkv_weight, qv_bias, out_weight, out_bias, norm2_gain, norm2_bias, up_weight, up_bias, down_weight, down_bias, cotangent, filled):
    params = (norm1_gain.astype(jnp.float32), norm1_bias.astype(jnp.float32), qkv_weight.astype(jnp.float32), qv_bias.astype(jnp.float32), out_weight.astype(jnp.float32), out_bias.astype(jnp.float32), norm2_gain.astype(jnp.float32), norm2_bias.astype(jnp.float32), up_weight.astype(jnp.float32), up_bias.astype(jnp.float32), down_weight.astype(jnp.float32), down_bias.astype(jnp.float32))
    flags = filled.astype(jnp.float32)

    def one_image(totals, item):
        image, image_cot, flag = item
        result, pull = jax.vjp(forward, params, image)
        param_grads, image_grad = pull(image_cot * flag)
        totals = jax.tree.map(lambda left, right: left + right, totals, param_grads)
        return (totals, (result.astype(jnp.bfloat16), image_grad.astype(jnp.bfloat16)))
    start = tuple((jnp.zeros_like(weight) for weight in params))
    totals, (output, input_grad) = lax.scan(one_image, start, (images.astype(jnp.float32), cotangent.astype(jnp.float32), flags))
    return (output, input_grad, totals[0], totals[1], totals[2], totals[3], totals[4], totals[5], totals[6], totals[7], totals[8], totals[9], totals[10], totals[11])
```

```python
import functools
import math

import jax
import jax.numpy as jnp
from jax import lax
from jax.experimental import pallas as pl
from jax.experimental.pallas import tpu as pltpu
from jax.sharding import PartitionSpec as P

HEADS = 16
HD = 64
LANES = 128
EPS = 1e-06
AXES = ("dev", "rep")
BF = jnp.bfloat16
F32 = jnp.float32


def mm(left, right):
    return jnp.dot(left, right, preferred_element_type=F32)


def mm_nt(left, right):
    return lax.dot_general(left, right, (((1,), (1,)), ((), ())), preferred_element_type=F32)


def mm_tn(left, right):
    return lax.dot_general(left, right, (((0,), (0,)), ((), ())), preferred_element_type=F32)


def head_masks(shape):
    lane = lax.broadcasted_iota(jnp.int32, shape, 1)
    return [(lane >= h * HD) & (lane < (h + 1) * HD) for h in range(LANES // HD)]


def attend_kernel(seq, scale, q_ref, k_ref, v_ref, out_ref, log_ref):
    queries = q_ref[...]
    keys = k_ref[...] * jnp.asarray(scale, BF)
    values = v_ref[...]
    rows = queries.shape[0]
    masks = head_masks(queries.shape)
    zero = jnp.zeros((), BF)
    total = None
    for h, mask in enumerate(masks):
        scores = mm_nt(jnp.where(mask, keys, zero), queries)
        row = lax.broadcasted_iota(jnp.int32, scores.shape, 0)
        scores = jnp.where(row < seq, scores, -1e30)
        highest = jnp.max(scores, axis=0, keepdims=True)
        raised = jnp.exp(scores - highest)
        sums = jnp.sum(raised, axis=0, keepdims=True)
        probs = (raised * (1.0 / sums)).astype(BF)
        mixed = mm_tn(probs, jnp.where(mask, values, zero))
        total = mixed if total is None else total + mixed
        log_ref[0, 0, h : h + 1, :] = highest + jnp.log(sums)
    out_ref[...] = total.astype(BF)


def attend_back_kernel(seq, scale, q_ref, k_ref, v_ref, g_ref, log_ref, dq_ref, dk_ref, dv_ref):
    queries = q_ref[...]
    keys = k_ref[...] * jnp.asarray(scale, BF)
    values = v_ref[...]
    grads = g_ref[...]
    masks = head_masks(queries.shape)
    zero = jnp.zeros((), BF)
    dq = dk = dv = None
    for h, mask in enumerate(masks):
        key_own = jnp.where(mask, keys, zero)
        scores = mm_nt(key_own, queries)
        row = lax.broadcasted_iota(jnp.int32, scores.shape, 0)
        probs = jnp.where(row < seq, jnp.exp(scores - log_ref[0, 0, h : h + 1, :]), 0.0)
        prob_grad = mm_nt(jnp.where(mask, values, zero), grads)
        share = jnp.sum(probs * prob_grad, axis=0, keepdims=True)
        score_low = (probs * (prob_grad - share)).astype(BF)
        dv_h = mm(probs.astype(BF), jnp.where(mask, grads, zero))
        dk_h = mm(score_low, jnp.where(mask, queries, zero))
        dq_h = mm_tn(score_low, key_own)
        dv = dv_h if dv is None else dv + dv_h
        dk = dk_h if dk is None else dk + dk_h
        dq = dq_h if dq is None else dq + dq_h
    dq_ref[...] = dq.astype(BF)
    dk_ref[...] = (dk * scale).astype(BF)
    dv_ref[...] = dv.astype(BF)


def attend(joined, images_now, rows, seq, scale):
    width = joined.shape[1] // 3
    pairs = width // LANES

    def part(which):
        return pl.BlockSpec((rows, LANES), lambda i, j: (i, which * pairs + j))

    heads = LANES // HD
    return pl.pallas_call(
        functools.partial(attend_kernel, seq, scale),
        grid=(images_now, pairs),
        in_specs=[part(0), part(1), part(2)],
        out_specs=[
            pl.BlockSpec((rows, LANES), lambda i, j: (i, j)),
            pl.BlockSpec((1, 1, heads, rows), lambda i, j: (i, j, 0, 0)),
        ],
        out_shape=[
            jax.ShapeDtypeStruct((images_now * rows, width), BF),
            jax.ShapeDtypeStruct((images_now, pairs, heads, rows), F32),
        ],
        compiler_params=pltpu.CompilerParams(vmem_limit_bytes=40 << 20),
        cost_estimate=pl.CostEstimate(
            flops=4 * images_now * HEADS * rows * rows * LANES * 2,
            bytes_accessed=images_now * rows * width * 8,
            transcendentals=images_now * HEADS * rows * rows,
        ),
        name="attend",
    )(joined, joined, joined)


def attend_back(joined, grads, logs, images_now, rows, seq, scale):
    width = joined.shape[1] // 3
    pairs = width // LANES
    heads = LANES // HD

    def part(which):
        return pl.BlockSpec((rows, LANES), lambda i, j: (i, which * pairs + j))

    own = pl.BlockSpec((rows, LANES), lambda i, j: (i, j))
    return pl.pallas_call(
        functools.partial(attend_back_kernel, seq, scale),
        grid=(images_now, pairs),
        in_specs=[
            part(0),
            part(1),
            part(2),
            own,
            pl.BlockSpec((1, 1, heads, rows), lambda i, j: (i, j, 0, 0)),
        ],
        out_specs=[own, own, own],
        out_shape=[jax.ShapeDtypeStruct((images_now * rows, width), BF)] * 3,
        compiler_params=pltpu.CompilerParams(vmem_limit_bytes=48 << 20),
        cost_estimate=pl.CostEstimate(
            flops=10 * images_now * HEADS * rows * rows * LANES * 2,
            bytes_accessed=images_now * rows * width * 14,
            transcendentals=images_now * HEADS * rows * rows,
        ),
        name="attend_back",
    )(joined, joined, joined, grads, logs)


def index_bits(sizes):
    dev, rep = sizes
    out = []
    for size, stride, axis in ((dev, rep, "dev"), (rep, 1, "rep")):
        for bit in reversed(range(size.bit_length() - 1)):
            step = stride << bit
            out.append((axis, bit, [(i, i ^ step) for i in range(dev * rep)]))
    return out


def scatter_sum(full, sizes, orders):
    bits = index_bits(sizes)
    count = sizes[0] * sizes[1]
    rows = full.shape[0] // count
    pieces = []
    cut = full.shape[1] // len(orders)
    for number, order in enumerate(orders):
        value = full[:, number * cut : (number + 1) * cut]
        value = value.reshape((2,) * len(bits) + (rows, cut))
        left = list(range(len(bits)))
        for which in order:
            axis, bit, flips = bits[which]
            place = left.index(which)
            mine = (lax.axis_index(axis) >> bit) & 1
            send = lax.dynamic_index_in_dim(value, 1 - mine, place, keepdims=False)
            keep = lax.dynamic_index_in_dim(value, mine, place, keepdims=False)
            value = keep + lax.ppermute(send, AXES, flips)
            left.remove(which)
        pieces.append(value.reshape(rows, cut))
    return jnp.concatenate(pieces, axis=1).astype(F32)


def norm_stats(values):
    centred = values - jnp.mean(values, axis=-1, keepdims=True)
    spread = jnp.mean(centred * centred, axis=-1, keepdims=True)
    inverse = lax.rsqrt(spread + EPS)
    return centred * inverse, inverse


def norm_back(normed, inverse, gain, grad):
    scaled = grad * gain
    return inverse * (
        scaled
        - jnp.mean(scaled, axis=-1, keepdims=True)
        - normed * jnp.mean(scaled * normed, axis=-1, keepdims=True)
    )


def gelu_and_slope(values):
    half = 0.5 * (1.0 + lax.erf(values * (1.0 / math.sqrt(2.0))))
    bell = jnp.exp(-0.5 * values * values) * (1.0 / math.sqrt(2.0 * math.pi))
    return values * half, half + values * bell


def body(sizes, *args):
    images, cotangent, filled = args[0], args[13], args[14]
    small_in = (args[1], args[2], args[4], args[6], args[7], args[8], args[10], args[12])
    big_in = (args[3], args[5], args[9], args[11])
    count = sizes[0] * sizes[1]
    images_now, seq, width = images.shape
    rows = -(-seq // 16) * 16
    tokens = images_now * rows
    scale = 1.0 / math.sqrt(HD)

    packed = lax.all_gather(jnp.concatenate(small_in), AXES, axis=0, tiled=False)
    packed = packed.reshape(count, -1)
    smalls, at = [], 0
    for one in small_in:
        smalls.append(packed[:, at : at + one.shape[0]].reshape(-1).astype(F32))
        at += one.shape[0]
    gain_one, bias_one, joint_bias, proj_bias, gain_two, bias_two, up_bias, down_bias = smalls
    joint_w, proj_w, up_w, down_w = [lax.all_gather(w, AXES, axis=0, tiled=True) for w in big_in]

    pad = ((0, 0), (0, rows - seq), (0, 0))
    residual_in = jnp.pad(images, pad).reshape(tokens, width).astype(F32)
    n_one, r_one = norm_stats(residual_in)
    normed_one = (n_one * gain_one + bias_one).astype(BF)
    bias_full = jnp.concatenate([joint_bias[:width], jnp.zeros((width,), F32), joint_bias[width:]])
    joined = (mm(normed_one, joint_w) + bias_full).astype(BF)
    heads_out, logs = attend(joined, images_now, rows, seq, scale)
    middle = residual_in + mm(heads_out, proj_w) + proj_bias
    n_two, r_two = norm_stats(middle)
    normed_two = (n_two * gain_two + bias_two).astype(BF)
    activated, slope = gelu_and_slope(mm(normed_two, up_w) + up_bias)
    activated = activated.astype(BF)
    slope = slope.astype(BF)
    output = (middle + mm(activated, down_w) + down_bias).astype(BF)
    output = output.reshape(images_now, rows, width)[:, :seq]

    flags = filled.astype(BF)[:, None, None]
    branch = jnp.pad(cotangent * flags, pad).reshape(tokens, width)
    out_grad = branch.astype(F32)
    orders = scatter_orders(sizes)
    down_grad = mm_tn(activated, branch).astype(BF)
    down_sum = scatter_sum(down_grad, sizes, orders)
    pre_grad = (mm_nt(branch, down_w) * slope).astype(BF)
    up_grad = mm_tn(normed_two, pre_grad).astype(BF)
    up_sum = scatter_sum(up_grad, sizes, orders)
    norm_two_in = mm_nt(pre_grad, up_w)
    middle_grad = out_grad + norm_back(n_two, r_two, gain_two, norm_two_in)
    attn_grad = middle_grad.astype(BF)
    proj_grad = mm_tn(heads_out, attn_grad).astype(BF)
    proj_sum = scatter_sum(proj_grad, sizes, orders)
    heads_grad = mm_nt(attn_grad, proj_w).astype(BF)
    dq, dk, dv = attend_back(joined, heads_grad, logs, images_now, rows, seq, scale)
    joined_grad = jnp.concatenate([dq, dk, dv], axis=1)
    joint_grad = mm_tn(normed_one, joined_grad).astype(BF)
    joint_sum = scatter_sum(joint_grad, sizes, orders)
    norm_one_in = mm_nt(joined_grad, joint_w)
    input_grad = (middle_grad + norm_back(n_one, r_one, gain_one, norm_one_in)).astype(BF)
    input_grad = input_grad.reshape(images_now, rows, width)[:, :seq]

    def over_tokens(value):
        return jnp.sum(value, axis=0, dtype=F32)

    joint_sums = over_tokens(joined_grad)
    small_grads = (
        over_tokens(norm_one_in * n_one),
        over_tokens(norm_one_in),
        jnp.concatenate([joint_sums[:width], joint_sums[2 * width :]]),
        over_tokens(attn_grad),
        over_tokens(norm_two_in * n_two),
        over_tokens(norm_two_in),
        over_tokens(pre_grad),
        over_tokens(branch),
    )
    stacked = jnp.concatenate([g.reshape(count, -1) for g in small_grads], axis=1)
    mine = lax.psum_scatter(stacked, AXES, scatter_dimension=0, tiled=True).reshape(-1)
    shares, at = [], 0
    for one in small_in:
        shares.append(mine[at : at + one.shape[0]])
        at += one.shape[0]
    return (
        output,
        input_grad,
        shares[0],
        shares[1],
        joint_sum,
        shares[2],
        proj_sum,
        shares[3],
        shares[4],
        shares[5],
        up_sum,
        shares[6],
        down_sum,
        shares[7],
    )


def scatter_orders(sizes):
    bits = len(index_bits(sizes))
    devs = sizes[0].bit_length() - 1
    reps = list(range(devs, bits))
    if devs < 3:
        return [list(range(bits))] * 2
    inner = list(range(devs - 3))
    y, x, core = devs - 3, devs - 2, devs - 1
    return [[core, x, y] + inner + reps, [core, y, x] + inner + reps]


def solution(mesh):
    sizes = (mesh.shape["dev"], mesh.shape["rep"])
    both = ("dev", "rep")
    three, one, two = P(both, None, None), P(both), P(both, None)
    in_specs = (three, one, one, two, one, two, one, one, one, two, one, two, one, three, one)
    out_specs = (three, three, one, one, two, one, two, one, one, one, two, one, two, one)
    return jax.shard_map(
        functools.partial(body, sizes),
        mesh=mesh,
        in_specs=in_specs,
        out_specs=out_specs,
        check_vma=False,
    )
```

```python
import functools
import heapq
import math

import jax
import jax.numpy as jnp
from jax import lax
from jax.experimental import pallas as pl
from jax.experimental.pallas import tpu as pltpu
from jax.sharding import PartitionSpec as P

HEADS = 16
HD = 64
MESH = pl.DeviceIdType.MESH
FAST_MESH = (8, 4)
GRID_STEPS = 16
STEP_US = {"attend": 2.2}
DEPTH = 4
LANES = 128
EPS = 1e-06
AXES = ("dev", "rep")
BF = jnp.bfloat16
F32 = jnp.float32


def mm(left, right):
    return jnp.dot(left, right, preferred_element_type=F32)


def mm_nt(left, right):
    return lax.dot_general(left, right, (((1,), (1,)), ((), ())), preferred_element_type=F32)


def mm_tn(left, right):
    return lax.dot_general(left, right, (((0,), (0,)), ((), ())), preferred_element_type=F32)


def head_masks(shape):
    lane = lax.broadcasted_iota(jnp.int32, shape, 1)
    return [(lane >= h * HD) & (lane < (h + 1) * HD) for h in range(LANES // HD)]


def attend_pair(seq, scale, q_ref, k_ref, v_ref, out_ref, log_ref):
    queries = q_ref[...]
    keys = k_ref[...] * jnp.asarray(scale, BF)
    values = v_ref[...]
    masks = head_masks(queries.shape)
    zero = jnp.zeros((), BF)
    total = None
    for h, mask in enumerate(masks):
        scores = mm_nt(jnp.where(mask, keys, zero), queries)
        row = lax.broadcasted_iota(jnp.int32, scores.shape, 0)
        scores = jnp.where(row < seq, scores, -1e30)
        highest = jnp.max(scores, axis=0, keepdims=True)
        raised = jnp.exp(scores - highest)
        sums = jnp.sum(raised, axis=0, keepdims=True)
        probs = (raised * (1.0 / sums)).astype(BF)
        mixed = mm_tn(probs, jnp.where(mask, values, zero))
        total = mixed if total is None else total + mixed
        log_ref[0, 0, h : h + 1, :] = highest + jnp.log(sums)
    out_ref[...] = total.astype(BF)


def attend_kernel(seq, scale, count, q_ref, k_ref, v_ref, *refs):
    shards, (out_ref, log_ref), fulls = refs[:count], refs[count : count + 2], refs[count + 2 : 2 * count + 2]
    compute = functools.partial(attend_pair, seq, scale, q_ref, k_ref, v_ref, out_ref, log_ref)
    if count == 0:
        compute()
        return
    send_sems, recv_sems, own_sems = refs[2 * count + 2 :]
    at = place()
    copies = Copies(at, send_sems, recv_sems)
    owns, steps = gather_plan(copies, shards, fulls, own_sems)

    def begin():
        greet(at)
        for own in owns:
            own().start()

    beside(compute, STEP_US["attend"], steps, begin, copies.drain)


def beside(compute, step_us, steps, first, last):
    now = pl.program_id(0) * pl.num_programs(1) + pl.program_id(1)
    ends = GRID_STEPS - 1
    groups = [[] for _ in range(GRID_STEPS)]
    for ready, run in steps:
        groups[min(ends, int(ready / step_us))].append(run)
    pl.when(now == 0)(first)
    for number, group in enumerate(groups[:-1]):
        if group:

            @pl.when(now == number)
            def _(group=group):
                for run in group:
                    run()

    compute()

    @pl.when(now == ends)
    def _():
        for run in groups[-1]:
            run()
        last()


def attend_back_kernel(seq, scale, q_ref, k_ref, v_ref, g_ref, log_ref, dq_ref, dk_ref, dv_ref):
    queries = q_ref[...]
    keys = k_ref[...] * jnp.asarray(scale, BF)
    values = v_ref[...]
    grads = g_ref[...]
    masks = head_masks(queries.shape)
    zero = jnp.zeros((), BF)
    dq = dk = dv = None
    for h, mask in enumerate(masks):
        key_own = jnp.where(mask, keys, zero)
        scores = mm_nt(key_own, queries)
        row = lax.broadcasted_iota(jnp.int32, scores.shape, 0)
        probs = jnp.where(row < seq, jnp.exp(scores - log_ref[0, 0, h : h + 1, :]), 0.0)
        prob_grad = mm_nt(jnp.where(mask, values, zero), grads)
        share = jnp.sum(probs * prob_grad, axis=0, keepdims=True)
        score_low = (probs * (prob_grad - share)).astype(BF)
        dv_h = mm(probs.astype(BF), jnp.where(mask, grads, zero))
        dk_h = mm(score_low, jnp.where(mask, queries, zero))
        dq_h = mm_tn(score_low, key_own)
        dv = dv_h if dv is None else dv + dv_h
        dk = dk_h if dk is None else dk + dk_h
        dq = dq_h if dq is None else dq + dq_h
    dq_ref[...] = dq.astype(BF)
    dk_ref[...] = (dk * scale).astype(BF)
    dv_ref[...] = dv.astype(BF)


def attend(joined, images_now, rows, seq, scale, shards=()):
    width = joined.shape[1] // 3
    pairs = width // LANES
    heads = LANES // HD
    count = len(shards)
    anywhere = pl.BlockSpec(memory_space=pl.ANY)

    def part(which):
        return pl.BlockSpec((rows, LANES), lambda i, j: (i, which * pairs + j))

    params = dict(vmem_limit_bytes=40 << 20)
    if count:
        params.update(collective_id=1, has_side_effects=True)
    return pl.pallas_call(
        functools.partial(attend_kernel, seq, scale, count),
        grid=(images_now, pairs),
        in_specs=[part(0), part(1), part(2)] + [anywhere] * count,
        out_specs=[
            pl.BlockSpec((rows, LANES), lambda i, j: (i, j)),
            pl.BlockSpec((1, 1, heads, rows), lambda i, j: (i, j, 0, 0)),
        ]
        + [anywhere] * count,
        out_shape=[
            jax.ShapeDtypeStruct((images_now * rows, width), BF),
            jax.ShapeDtypeStruct((images_now, pairs, heads, rows), F32),
        ]
        + gathered_shapes(shards),
        scratch_shapes=gather_scratch(shards) if count else [],
        compiler_params=pltpu.CompilerParams(**params),
        cost_estimate=pl.CostEstimate(
            flops=4 * images_now * HEADS * rows * rows * LANES * 2,
            bytes_accessed=images_now * rows * width * 8,
            transcendentals=images_now * HEADS * rows * rows,
        ),
        name="attend",
    )(joined, joined, joined, *shards)


def attend_back(joined, grads, logs, images_now, rows, seq, scale):
    width = joined.shape[1] // 3
    pairs = width // LANES
    heads = LANES // HD

    def part(which):
        return pl.BlockSpec((rows, LANES), lambda i, j: (i, which * pairs + j))

    own = pl.BlockSpec((rows, LANES), lambda i, j: (i, j))
    return pl.pallas_call(
        functools.partial(attend_back_kernel, seq, scale),
        grid=(images_now, pairs),
        in_specs=[
            part(0),
            part(1),
            part(2),
            own,
            pl.BlockSpec((1, 1, heads, rows), lambda i, j: (i, j, 0, 0)),
        ],
        out_specs=[own, own, own],
        out_shape=[jax.ShapeDtypeStruct((images_now * rows, width), BF)] * 3,
        compiler_params=pltpu.CompilerParams(vmem_limit_bytes=48 << 20),
        cost_estimate=pl.CostEstimate(
            flops=10 * images_now * HEADS * rows * rows * LANES * 2,
            bytes_accessed=images_now * rows * width * 14,
            transcendentals=images_now * HEADS * rows * rows,
        ),
        name="attend_back",
    )(joined, joined, joined, grads, logs)


ORDERS = (("x", "z", "y"), ("y", "z", "x"), ("z", "x", "y"), ("z", "y", "x"))
SHARES = (8, 8, 4, 4)


def place():
    dev = lax.axis_index("dev")
    return dict(
        core=dev % 2, x=(dev // 2) % 2, y=dev // 4, z=lax.axis_index("rep")
    )


def peer(at, axis, step=0):
    other = dict(at)
    other[axis] = at[axis] + step if axis == "z" else 1 - at[axis]
    return {"dev": (other["y"] * 2 + other["x"]) * 2 + other["core"], "rep": other["z"]}


def greet(at):
    barrier = pltpu.get_barrier_semaphore()
    for axis in ("core", "x", "y"):
        pl.semaphore_signal(barrier, 1, device_id=peer(at, axis), device_id_type=MESH)
    for step in (1, -1):

        @pl.when((at["z"] + step >= 0) & (at["z"] + step < DEPTH))
        def _():
            pl.semaphore_signal(barrier, 1, device_id=peer(at, "z", step), device_id_type=MESH)

    ends = (at["z"] == 0) | (at["z"] == DEPTH - 1)

    @pl.when(ends)
    def _():
        pl.semaphore_wait(barrier, 4)

    @pl.when(jnp.logical_not(ends))
    def _():
        pl.semaphore_wait(barrier, 5)


def cuts(columns):
    units = columns // 128
    total = sum(SHARES)
    out, at, seen = [], 0, 0
    for order, share in zip(ORDERS, SHARES):
        seen += share
        end = round(units * seen / total)
        if end > at:
            out.append((order, at * 128, (end - at) * 128))
        at = end
    return out


class Copy:
    def __init__(self, owner, number, source, target, axis, step, sends, comes):
        self.owner, self.number, self.source, self.target = owner, number, source, target
        self.axis, self.step, self.sends, self.comes = axis, step, sends, comes

    def build(self):
        return pltpu.make_async_remote_copy(
            src_ref=self.source(),
            dst_ref=self.target(),
            send_sem=self.owner.send_sems.at[self.number],
            recv_sem=self.owner.recv_sems.at[self.number],
            device_id=peer(self.owner.at, self.axis, self.step),
            device_id_type=MESH,
        )

    def guarded(self, condition, act):
        if condition is None:
            act()
        else:
            pl.when(condition())(act)

    def start(self):
        self.guarded(self.sends, lambda: self.build().start())

    def wait_send(self):
        self.guarded(self.sends, lambda: self.build().wait_send())

    def wait_recv(self):
        self.guarded(self.comes, lambda: self.build().wait_recv())


class Copies:
    def __init__(self, at, send_sems, recv_sems):
        self.at, self.send_sems, self.recv_sems = at, send_sems, recv_sems
        self.all = []

    def make(self, source, target, axis, step=0, sends=None, comes=None):
        copy = Copy(self, len(self.all), source, target, axis, step, sends, comes)
        self.all.append(copy)
        return copy

    def drain(self):
        for copy in self.all:
            copy.wait_send()


LINK = {"x": 90.0, "y": 90.0, "zr": 90.0, "zl": 90.0, "core": 600.0}


def issue_order(chains):
    free = dict.fromkeys(LINK, 0.0)
    queue = [(0.0, number, 0) for number in range(len(chains))]
    heapq.heapify(queue)
    out = []
    while queue:
        ready, number, step = heapq.heappop(queue)
        links, size, run = chains[number][step]
        out.append((ready, run))
        done = ready
        for link in links:
            begin = max(free[link], ready)
            free[link] = begin + size / LINK[link]
            done = max(done, free[link] + 2.0)
        if step + 1 < len(chains[number]):
            heapq.heappush(queue, (done, number, step + 1))
    return out


def on_line(at, direction, hop):
    def sends():
        source, target = at["z"] - direction * (hop - 1), at["z"] + direction
        return (source >= 0) & (source < DEPTH) & (target >= 0) & (target < DEPTH)

    def comes():
        source = at["z"] - direction * hop
        return (source >= 0) & (source < DEPTH)

    return sends, comes


def gather_chain(copies, shard, full, order, columns, own_ready):
    at = copies.at
    steps = []
    begin, width = columns
    size = 2 * full.shape[4] * width * 2 / 1000.0
    pending = []

    def region(held, block_z=None):
        def along(axis, extent):
            return pl.ds(0, extent) if axis in held else at[axis]

        z = pl.ds(0, DEPTH) if "z" in held else (at["z"] if block_z is None else block_z)
        y, x = along("y", full.shape[0]), along("x", full.shape[1])
        return full.at[y, x, at["core"], z, :, pl.ds(begin, width)]

    def step(links, size, copies_now, own=False):
        before = list(pending)
        pending.clear()
        pending.extend(copies_now)

        def run():
            if own:
                own_ready()
            for copy in before:
                copy.wait_recv()
            for copy in copies_now:
                copy.start()

        steps.append((links, size, run))

    def first():
        return shard.at[:, pl.ds(begin, width)]

    held, blocks = (), 1
    for axis in order:
        here = functools.partial(region, held)
        if axis == "z":
            for hop in range(1, DEPTH):
                now = []
                for direction in (1, -1):

                    def place_of(direction=direction, hop=hop, here=here):
                        return here(at["z"] - direction * (hop - 1))

                    source = first if blocks == 1 and hop == 1 else place_of
                    sends, comes = on_line(at, direction, hop)
                    now.append(copies.make(source, place_of, "z", direction, sends, comes))
                step(("zr", "zl"), size * blocks, now, blocks > 1 and hop == 1)
            blocks *= DEPTH
        else:
            copy = copies.make(first if blocks == 1 else here, here, axis)
            step((axis,), size * blocks, [copy], blocks > 1)
            blocks *= 2
        held += (axis,)
    whole = functools.partial(region, held)
    step(("core",), size * blocks / 2, [copies.make(whole, whole, "core")])
    step((), 0.0, [])
    return steps


def gather_plan(copies, shards, fulls, own_sems):
    at = copies.at
    chains, owns = [], []
    for number, (shard, full) in enumerate(zip(shards, fulls)):

        def own(number=number, shard=shard, full=full):
            mine = full.at[at["y"], at["x"], at["core"], at["z"]]
            return pltpu.make_async_copy(shard, mine, own_sems.at[number])

        owns.append(own)
        waited = []

        def ready(own=own, waited=waited):
            if not waited:
                own().wait()
                waited.append(True)

        if full.shape[4] > 1:
            parts = cuts(full.shape[5])
        else:
            parts = [(ORDERS[0], 0, full.shape[5])]
        for order, begin, width in parts:
            chains.append(gather_chain(copies, shard, full, order, (begin, width), ready))
    return owns, issue_order(chains)


def gathered_shapes(shards):
    return [jax.ShapeDtypeStruct((2, 2, 2, DEPTH) + s.shape, s.dtype) for s in shards]


def gather_scratch(shards):
    count = 9 * sum(len(cuts(s.shape[1])) if s.shape[0] > 1 else 1 for s in shards)
    return [
        pltpu.SemaphoreType.DMA((count,)),
        pltpu.SemaphoreType.DMA((count,)),
        pltpu.SemaphoreType.DMA((len(shards),)),
    ]


def gather_kernel(count, *refs):
    shards, fulls = refs[:count], refs[count : 2 * count]
    send_sems, recv_sems, own_sems = refs[2 * count :]
    at = place()
    greet(at)
    copies = Copies(at, send_sems, recv_sems)
    owns, steps = gather_plan(copies, shards, fulls, own_sems)
    for own in owns:
        own().start()
    for _, run in steps:
        run()
    copies.drain()


def gather(shards, number):
    count = len(shards)
    anywhere = pl.BlockSpec(memory_space=pl.ANY)
    return pl.pallas_call(
        functools.partial(gather_kernel, count),
        in_specs=[anywhere] * count,
        out_specs=[anywhere] * count,
        out_shape=gathered_shapes(shards),
        scratch_shapes=gather_scratch(shards),
        compiler_params=pltpu.CompilerParams(
            collective_id=number, has_side_effects=True, vmem_limit_bytes=16 << 20
        ),
        name="gather_weights",
    )(*shards)


def index_bits(sizes):
    dev, rep = sizes
    out = []
    for size, stride, axis in ((dev, rep, "dev"), (rep, 1, "rep")):
        for bit in reversed(range(size.bit_length() - 1)):
            step = stride << bit
            out.append((axis, bit, [(i, i ^ step) for i in range(dev * rep)]))
    return out


def scatter_sum(full, sizes, orders):
    bits = index_bits(sizes)
    count = sizes[0] * sizes[1]
    rows = full.shape[0] // count
    pieces = []
    cut = full.shape[1] // len(orders)
    for number, order in enumerate(orders):
        value = full[:, number * cut : (number + 1) * cut]
        value = value.reshape((2,) * len(bits) + (rows, cut))
        left = list(range(len(bits)))
        for which in order:
            axis, bit, flips = bits[which]
            place = left.index(which)
            mine = (lax.axis_index(axis) >> bit) & 1
            send = lax.dynamic_index_in_dim(value, 1 - mine, place, keepdims=False)
            keep = lax.dynamic_index_in_dim(value, mine, place, keepdims=False)
            value = keep + lax.ppermute(send, AXES, flips)
            left.remove(which)
        pieces.append(value.reshape(rows, cut))
    return jnp.concatenate(pieces, axis=1).astype(F32)


def norm_stats(values):
    centred = values - jnp.mean(values, axis=-1, keepdims=True)
    spread = jnp.mean(centred * centred, axis=-1, keepdims=True)
    inverse = lax.rsqrt(spread + EPS)
    return centred * inverse, inverse


def norm_back(normed, inverse, gain, grad):
    scaled = grad * gain
    return inverse * (
        scaled
        - jnp.mean(scaled, axis=-1, keepdims=True)
        - normed * jnp.mean(scaled * normed, axis=-1, keepdims=True)
    )


def gelu_and_slope(values):
    half = 0.5 * (1.0 + lax.erf(values * (1.0 / math.sqrt(2.0))))
    bell = jnp.exp(-0.5 * values * values) * (1.0 / math.sqrt(2.0 * math.pi))
    return values * half, half + values * bell


def body(sizes, *args):
    images, cotangent, filled = args[0], args[13], args[14]
    small_in = (args[1], args[2], args[4], args[6], args[7], args[8], args[10], args[12])
    big_in = (args[3], args[5], args[9], args[11])
    count = sizes[0] * sizes[1]
    images_now, seq, width = images.shape
    rows = -(-seq // 16) * 16
    tokens = images_now * rows
    scale = 1.0 / math.sqrt(HD)

    fast = sizes == FAST_MESH
    joint_shard, proj_shard, up_shard, down_shard = big_in
    packed = jnp.concatenate(small_in)[None]
    if fast:
        packed, joint_w = gather((packed, joint_shard), 0)
        joint_w = joint_w.reshape(count * joint_shard.shape[0], -1)
        later = (proj_shard, up_shard, down_shard)
    else:
        packed = lax.all_gather(packed, AXES, axis=0, tiled=False)
        joint_w, proj_w, up_w, down_w = [lax.all_gather(w, AXES, axis=0, tiled=True) for w in big_in]
        later = ()
    packed = packed.reshape(count, -1)
    smalls, at = [], 0
    for one in small_in:
        smalls.append(packed[:, at : at + one.shape[0]].reshape(-1).astype(F32))
        at += one.shape[0]
    gain_one, bias_one, joint_bias, proj_bias, gain_two, bias_two, up_bias, down_bias = smalls

    pad = ((0, 0), (0, rows - seq), (0, 0))
    residual_in = jnp.pad(images, pad).reshape(tokens, width).astype(F32)
    n_one, r_one = norm_stats(residual_in)
    normed_one = (n_one * gain_one + bias_one).astype(BF)
    bias_full = jnp.concatenate([joint_bias[:width], jnp.zeros((width,), F32), joint_bias[width:]])
    joined = (mm(normed_one, joint_w) + bias_full).astype(BF)
    heads_out, logs, *found = attend(joined, images_now, rows, seq, scale, later)
    if fast:
        proj_w, up_w, down_w = [
            full.reshape(count * shard.shape[0], -1) for full, shard in zip(found, later)
        ]
    middle = residual_in + mm(heads_out, proj_w) + proj_bias
    n_two, r_two = norm_stats(middle)
    normed_two = (n_two * gain_two + bias_two).astype(BF)
    activated, slope = gelu_and_slope(mm(normed_two, up_w) + up_bias)
    activated = activated.astype(BF)
    slope = slope.astype(BF)
    output = (middle + mm(activated, down_w) + down_bias).astype(BF)
    output = output.reshape(images_now, rows, width)[:, :seq]

    flags = filled.astype(BF)[:, None, None]
    branch = jnp.pad(cotangent * flags, pad).reshape(tokens, width)
    out_grad = branch.astype(F32)
    orders = scatter_orders(sizes)
    down_grad = mm_tn(activated, branch).astype(BF)
    down_sum = scatter_sum(down_grad, sizes, orders)
    pre_grad = (mm_nt(branch, down_w) * slope).astype(BF)
    up_grad = mm_tn(normed_two, pre_grad).astype(BF)
    up_sum = scatter_sum(up_grad, sizes, orders)
    norm_two_in = mm_nt(pre_grad, up_w)
    middle_grad = out_grad + norm_back(n_two, r_two, gain_two, norm_two_in)
    attn_grad = middle_grad.astype(BF)
    proj_grad = mm_tn(heads_out, attn_grad).astype(BF)
    proj_sum = scatter_sum(proj_grad, sizes, orders)
    heads_grad = mm_nt(attn_grad, proj_w).astype(BF)
    dq, dk, dv = attend_back(joined, heads_grad, logs, images_now, rows, seq, scale)
    joined_grad = jnp.concatenate([dq, dk, dv], axis=1)
    joint_grad = mm_tn(normed_one, joined_grad).astype(BF)
    joint_sum = scatter_sum(joint_grad, sizes, orders)
    norm_one_in = mm_nt(joined_grad, joint_w)
    input_grad = (middle_grad + norm_back(n_one, r_one, gain_one, norm_one_in)).astype(BF)
    input_grad = input_grad.reshape(images_now, rows, width)[:, :seq]

    def over_tokens(value):
        return jnp.sum(value, axis=0, dtype=F32)

    joint_sums = over_tokens(joined_grad)
    small_grads = (
        over_tokens(norm_one_in * n_one),
        over_tokens(norm_one_in),
        jnp.concatenate([joint_sums[:width], joint_sums[2 * width :]]),
        over_tokens(attn_grad),
        over_tokens(norm_two_in * n_two),
        over_tokens(norm_two_in),
        over_tokens(pre_grad),
        over_tokens(branch),
    )
    stacked = jnp.concatenate([g.reshape(count, -1) for g in small_grads], axis=1)
    mine = lax.psum_scatter(stacked, AXES, scatter_dimension=0, tiled=True).reshape(-1)
    shares, at = [], 0
    for one in small_in:
        shares.append(mine[at : at + one.shape[0]])
        at += one.shape[0]
    return (
        output,
        input_grad,
        shares[0],
        shares[1],
        joint_sum,
        shares[2],
        proj_sum,
        shares[3],
        shares[4],
        shares[5],
        up_sum,
        shares[6],
        down_sum,
        shares[7],
    )


def scatter_orders(sizes):
    bits = len(index_bits(sizes))
    devs = sizes[0].bit_length() - 1
    reps = list(range(devs, bits))
    if devs < 3:
        return [list(range(bits))] * 2
    inner = list(range(devs - 3))
    y, x, core = devs - 3, devs - 2, devs - 1
    return [[core, x, y] + inner + reps, [core, y, x] + inner + reps]


def solution(mesh):
    sizes = (mesh.shape["dev"], mesh.shape["rep"])
    both = ("dev", "rep")
    three, one, two = P(both, None, None), P(both), P(both, None)
    in_specs = (three, one, one, two, one, two, one, one, one, two, one, two, one, three, one)
    out_specs = (three, three, one, one, two, one, two, one, one, one, two, one, two, one)
    return jax.shard_map(
        functools.partial(body, sizes),
        mesh=mesh,
        in_specs=in_specs,
        out_specs=out_specs,
        check_vma=False,
    )
```

```python
import functools
import heapq
import math

import jax
import jax.numpy as jnp
from jax import lax
from jax.experimental import pallas as pl
from jax.experimental.pallas import tpu as pltpu
from jax.sharding import PartitionSpec as P

HEADS = 16
HD = 64
MESH = pl.DeviceIdType.MESH
FAST_MESH = (8, 4)
MLP_STEPS = 8
GROUPS = 1
TURNS = 2
RELEASES = ((0.0,), 28.0, 32.0, 60.0)
VMEM_LIMIT = 61 << 20
DEPTH = 4
LANES = 128
EPS = 1e-06
AXES = ("dev", "rep")
BF = jnp.bfloat16
F32 = jnp.float32


def mm(left, right):
    return jnp.dot(left, right, preferred_element_type=F32)


def mm_nt(left, right):
    return lax.dot_general(left, right, (((1,), (1,)), ((), ())), preferred_element_type=F32)


def mm_tn(left, right):
    return lax.dot_general(left, right, (((0,), (0,)), ((), ())), preferred_element_type=F32)


def head_masks(shape):
    lane = lax.broadcasted_iota(jnp.int32, shape, 1)
    return [(lane >= h * HD) & (lane < (h + 1) * HD) for h in range(LANES // HD)]


def attend_head(seq, scale, mask, queries, keys, values):
    zero = jnp.zeros((), BF)
    scores = mm_nt(jnp.where(mask, keys * jnp.asarray(scale, BF), zero), queries)
    row = lax.broadcasted_iota(jnp.int32, scores.shape, 0)
    scores = jnp.where(row < seq, scores, -1e30)
    highest = jnp.max(scores, axis=0, keepdims=True)
    raised = jnp.exp(scores - highest)
    sums = jnp.sum(raised, axis=0, keepdims=True)
    probs = (raised * (1.0 / sums)).astype(BF)
    mixed = mm_tn(probs, jnp.where(mask, values, zero))
    return mixed.astype(BF), highest + jnp.log(sums)


def attend_head_back(seq, scale, mask, queries, keys, values, grads, logs):
    zero = jnp.zeros((), BF)
    key_own = jnp.where(mask, keys * jnp.asarray(scale, BF), zero)
    scores = mm_nt(key_own, queries)
    row = lax.broadcasted_iota(jnp.int32, scores.shape, 0)
    probs = jnp.where(row < seq, jnp.exp(scores - logs), 0.0)
    prob_grad = mm_nt(jnp.where(mask, values, zero), grads)
    share = jnp.sum(probs * prob_grad, axis=0, keepdims=True)
    score_low = (probs * (prob_grad - share)).astype(BF)
    dv = mm(probs.astype(BF), jnp.where(mask, grads, zero))
    dk = mm(score_low, jnp.where(mask, queries, zero)) * scale
    dq = mm_tn(score_low, key_own)
    return dq.astype(BF), dk.astype(BF), dv.astype(BF)


class Beside:
    def __init__(self, now, slots, events=(), begin_us=0.0, earliest=None, latest=None):
        self.now, self.groups = now, {}
        keys = [slot[:2] for slot in slots]
        for ready, tag, run in events:
            left, index = ready - begin_us, 0
            while index < len(slots) - 1 and left >= slots[index][2]:
                left -= slots[index][2]
                index += 1
            if latest and tag in latest:
                index = min(index, keys.index(latest[tag]))
            if earliest and tag in earliest:
                index = max(index, keys.index(earliest[tag]))
            self.groups.setdefault(keys[index], []).append(run)
        for key in keys:
            self.groups[key] = [prepare() for prepare in self.groups.get(key, ())]

    def run(self, step, stage):
        for event in self.groups.get((step, stage), ()):
            event()

    def at(self, first, end, stage):
        for step in range(first, end):
            if self.groups.get((step, stage)):
                pl.when(self.now == step)(functools.partial(self.run, step, stage))


def slot_start(slots, key):
    out = 0.0
    for step, stage, length in slots:
        if (step, stage) == key:
            return out
        out += length
    return out


SMALL_AT = (0, 1, 2, 4, 5, 6, 7, 11)


def forward_slots(pairs_now):
    slots = []
    for step in range(pairs_now):
        slots += [(step, 0, 0.9), (step, 1, 1.1), (step, 2, 1.1)]
    slots.append((pairs_now, 0, 7.0))
    for step in range(pairs_now + 1, pairs_now + 1 + MLP_STEPS):
        slots += [(step, 0, 2.0), (step, 1, 1.6)]
    return slots


def forward_kernel(seq, rows, scale, count, shapes, *refs):
    refs = list(refs)

    def take(number):
        out = refs[:number]
        del refs[:number]
        return out

    images, cotangent, filled = take(3)
    if count:
        small_shards, shards = take(len(SMALL_AT)), take(count)
    else:
        (smalls,), fulls = take(1), take(3)
    q_ref, k_ref, v_ref, log_ref, branch, heads, n_one, middle, n_two = take(9)
    act_ref, slope_ref, grad_ref = take(3)
    if count:
        (smalls,), fulls = take(1), take(count)
    joint_tile, proj_all, up_tile, joint_sems, proj_sem, up_sems = take(6)
    images_now, width = images.shape[0], images.shape[2]
    pairs = width // LANES
    pairs_now = images_now * pairs
    joint, proj, up = fulls[:3]
    units = up.shape[5]
    tile = units // MLP_STEPS
    now = pl.program_id(0)
    last = pairs_now + MLP_STEPS

    def joint_load(pair, part):
        column = pl.multiple_of(part * width + pair * LANES, LANES)
        return pltpu.make_async_copy(
            joint.at[:, :, :, :, :, pl.ds(column, LANES)],
            joint_tile.at[pair % 2, part],
            joint_sems.at[pair % 2, part],
        )

    def proj_load():
        return pltpu.make_async_copy(proj, proj_all, proj_sem.at[0])

    def up_load(step):
        column = pl.multiple_of(step * tile, LANES)
        return pltpu.make_async_copy(
            up.at[:, :, :, :, :, pl.ds(column, tile)], up_tile.at[step % 2], up_sems.at[step % 2]
        )

    def first_norm():
        for image in range(images_now):
            normed, _ = norm_stats(images[image].astype(F32))
            low = (normed * smalls[0:1] + smalls[1:2]).astype(BF)
            n_one[image * rows : image * rows + seq] = low
            n_one[image * rows + seq : (image + 1) * rows] = jnp.zeros((rows - seq, width), BF)

    def mask_cotangent():
        for image in range(images_now):
            flag = filled[image].astype(F32)
            given = (cotangent[image].astype(F32) * flag).astype(BF)
            branch[image * rows : image * rows + seq] = given
            branch[image * rows + seq : (image + 1) * rows] = jnp.zeros((rows - seq, width), BF)

    slots = forward_slots(pairs_now)
    beside = Beside(now, slots)
    if count:
        held, found, send_sems, recv_sems, own_sems = take(5)
        at = place()
        copies = Copies(at, send_sems, recv_sems)
        owns, chains = gather_chains(copies, shards, fulls, own_sems, RELEASES)
        chains.insert(0, (0.0, "small", small_chain(copies, held, found, smalls)))
        events = issue_order(chains)
        urgent = max(i for i, event in enumerate(events) if event[1] in ("small", (0, 0)))
        norm_after = max(i for i, event in enumerate(events) if event[1] == "small")
        due = {1: (pairs_now - 1, 2), 2: (pairs_now, 0)}
        for group in range(1, GROUPS):
            due[0, group] = ((group * pairs // GROUPS - 1) * images_now, 0)
        first_runs = [prepare() for _, _, prepare in events[: urgent + 1]]
        beside = Beside(now, slots, events[urgent + 1 :], events[urgent][0], None, due)

    @pl.when(now == 0)
    def _():
        if count:
            greet(at)
            for own in owns:
                own().start()
            mine = (at["y"] * 2 + at["x"]) * 2 + at["core"]
            mine = mine * DEPTH + at["z"]
            held[0] = jnp.zeros(held.shape[1:], F32)
            for shard, row in zip(small_shards, SMALL_AT):
                size = shard.shape[1]
                whole = size * 8 * DEPTH
                spot = lax.broadcasted_iota(jnp.int32, (size, whole), 0) + mine * size
                hot = lax.broadcasted_iota(jnp.int32, (size, whole), 1) == spot
                piece = mm(shard[...], jnp.where(hot, 1.0, 0.0).astype(BF))
                for part in range(whole // width):
                    held[0, row + part : row + part + 1] = piece[:, part * width : (part + 1) * width]
            for number, run in enumerate(first_runs):
                run()
                if number == norm_after - 2:
                    mask_cotangent()
                if number == norm_after:
                    first_norm()
        else:
            mask_cotangent()
            first_norm()
        for part in range(3):
            joint_load(0, part).start()

    beside.at(0, pairs_now, 0)

    pair, image_now = now // images_now, now % images_now

    @pl.when((now < pairs_now) & (image_now == 0))
    def _():
        for part in range(3):
            joint_load(pair, part).wait()

        @pl.when(pair + 1 < pairs)
        def _():
            for part in range(3):
                joint_load(pair + 1, part).start()

    here = pl.ds(pl.multiple_of(image_now * rows, 16), rows)
    lanes = pl.ds(pl.multiple_of(pair % pairs * LANES, LANES), LANES)

    @pl.when(now < pairs_now)
    def _():
        own = n_one[here, :]
        for part, ref in enumerate((q_ref, k_ref, v_ref)):
            value = mm(own, joint_tile[pair % 2, part].reshape(width, LANES))
            if part != 1:
                value = value + smalls[2 + part // 2 : 3 + part // 2, lanes]
            ref[...] = value.astype(BF)

    for head in range(LANES // HD):
        beside.at(0, pairs_now, 1 + head)

        @pl.when(now < pairs_now)
        def _(head=head):
            mask = head_masks((rows, LANES))[head]
            mixed, logs = attend_head(seq, scale, mask, q_ref[...], k_ref[...], v_ref[...])
            heads[here, lanes] = mixed if head == 0 else heads[here, lanes] + mixed
            log_ref[0, 0, head : head + 1, :] = logs

    @pl.when(now == pairs_now - 1)
    def _():
        proj_load().start()

    beside.at(pairs_now, pairs_now + 1, 0)

    @pl.when(now == pairs_now)
    def _():
        up_load(0).start()
        proj_load().wait()
        for image in range(images_now):
            here = slice(image * rows, (image + 1) * rows)
            mixed = mm(heads[here], proj_all[...].reshape(width, width)) + smalls[4:5]
            middle[here] = mixed
            inner = slice(image * rows, image * rows + seq)
            middle[inner] = middle[inner] + images[image].astype(F32)
            normed, _ = norm_stats(middle[here])
            n_two[here] = (normed * smalls[5:6] + smalls[6:7]).astype(BF)

    beside.at(pairs_now + 1, last + 1, 0)

    @pl.when(now > pairs_now)
    def _():
        step = now - pairs_now - 1
        up_load(step).wait()

        @pl.when(step + 1 < MLP_STEPS)
        def _():
            up_load(step + 1).start()

        per_row = width // tile
        bias = smalls[
            pl.ds(7 + step // per_row, 1), pl.ds(pl.multiple_of(step % per_row * tile, LANES), tile)
        ]
        value = mm(n_two[...], up_tile[step % 2].reshape(width, tile)) + bias
        activated, slope = gelu_and_slope(value)
        act_ref[...] = activated.astype(BF)
        slope_ref[...] = slope.astype(BF)

    beside.at(pairs_now + 1, last + 1, 1)

    @pl.when(now > pairs_now)
    def _():
        grad_ref[...] = mm_tn(act_ref[...], branch[...]).astype(BF)

    if count:

        @pl.when(now == last)
        def _():
            copies.drain()


def forward(images, cotangent, filled, rows, seq, scale, smalls, weights):
    images_now, _, width = images.shape
    tokens = images_now * rows
    pairs = width // LANES
    pairs_now = images_now * pairs
    heads = LANES // HD
    shards = list(weights) if isinstance(smalls, tuple) else []
    count = len(shards)
    wide = weights[2].shape[1]
    tile = wide // MLP_STEPS
    block = width // (8 * DEPTH)
    anywhere = pl.BlockSpec(memory_space=pl.ANY)
    once = pl.Buffered(1)
    steps = pairs_now + 1 + MLP_STEPS

    def whole(shape):
        return pl.BlockSpec(shape, lambda s: (0,) * len(shape), pipeline_mode=once)

    def pair_at(s):
        s = jnp.minimum(s, pairs_now - 1)
        return s % images_now, s // images_now

    def tile_at(s):
        return jnp.clip(s - pairs_now - 1, 0, MLP_STEPS - 1)

    part = pl.BlockSpec((rows, LANES), pair_at)
    columns = pl.BlockSpec((tokens, tile), lambda s: (0, tile_at(s)))
    in_specs = [whole(images.shape), whole(images.shape), pl.BlockSpec(memory_space=pltpu.SMEM)]
    inputs = [images, cotangent, filled]
    if count:
        small_in = [v[None] for v in smalls]
        inputs += small_in + shards
        in_specs += [whole(v.shape) for v in small_in] + [anywhere] * count
    else:
        inputs += [smalls] + [w.reshape(2, 2, 2, DEPTH, block, -1) for w in weights[:3]]
        in_specs += [whole(smalls.shape)] + [anywhere] * 3
    out_specs = [
        part,
        part,
        part,
        pl.BlockSpec((1, 1, heads, rows), lambda s: pair_at(s) + (0, 0)),
        whole((tokens, width)),
        whole((tokens, width)),
        whole((tokens, width)),
        whole((tokens, width)),
        whole((tokens, width)),
        columns,
        columns,
        pl.BlockSpec((tile, width), lambda s: (tile_at(s), 0)),
    ]
    low = jax.ShapeDtypeStruct((tokens, width), BF)
    out_shape = [
        low,
        low,
        low,
        jax.ShapeDtypeStruct((images_now, pairs, heads, rows), F32),
        low,
        low,
        low,
        jax.ShapeDtypeStruct((tokens, width), F32),
        low,
        jax.ShapeDtypeStruct((tokens, wide), BF),
        jax.ShapeDtypeStruct((tokens, wide), BF),
        jax.ShapeDtypeStruct((wide, width), BF),
    ]
    parts = (2, 2, 2, DEPTH, block)
    scratch = [
        pltpu.VMEM((2, 3) + parts + (LANES,), BF),
        pltpu.VMEM(parts + (width,), BF),
        pltpu.VMEM((2,) + parts + (tile,), BF),
        pltpu.SemaphoreType.DMA((2, 3)),
        pltpu.SemaphoreType.DMA((1,)),
        pltpu.SemaphoreType.DMA((2,)),
    ]
    params = dict(vmem_limit_bytes=VMEM_LIMIT)
    if count:
        out_specs += [whole((SMALL_ROWS, width))] + [anywhere] * count
        out_shape += [jax.ShapeDtypeStruct((SMALL_ROWS, width), F32)] + gathered_shapes(shards)
        copies = SMALL_COPIES + 6 * (4 * GROUPS + sum(len(cuts(s.shape[1])) for s in shards[1:]))
        scratch += small_scratch() + [
            pltpu.SemaphoreType.DMA((copies,)),
            pltpu.SemaphoreType.DMA((copies,)),
            pltpu.SemaphoreType.DMA((count,)),
        ]
        params.update(collective_id=1, has_side_effects=True)
    matmuls = 2 * tokens * width * (4 * width + 2 * wide)
    return pl.pallas_call(
        functools.partial(forward_kernel, seq, rows, scale, count, None),
        grid=(steps,),
        in_specs=in_specs,
        out_specs=out_specs,
        out_shape=out_shape,
        scratch_shapes=scratch,
        compiler_params=pltpu.CompilerParams(**params),
        cost_estimate=pl.CostEstimate(
            flops=matmuls + 4 * images_now * HEADS * rows * rows * LANES * 2,
            bytes_accessed=tokens * width * 24 + tokens * wide * 4 + width * width * 30,
            transcendentals=images_now * HEADS * rows * rows + 2 * tokens * wide,
        ),
        name="forward",
    )(*inputs)


def middle_slots():
    slots = []
    for step in range(MLP_STEPS):
        slots += [(step, 0, 1.9), (step, 1, 1.7), (step, 2, 1.7), (step, 3, 1.7)]
    return slots + [(MLP_STEPS, 0, 2.5), (MLP_STEPS, 1, 2.5), (MLP_STEPS + 1, 0, 2.5), (MLP_STEPS + 1, 1, 2.5)]


def middle_kernel(rows, count, *refs):
    refs = list(refs)

    def take(number):
        out = refs[:number]
        del refs[:number]
        return out

    branch, act_tile, slope_tile, down_tile, up_tile, n_two, heads, proj, smalls, middle = take(10)
    grads = take(count)
    up_grad, output, norm_in, heads_grad, proj_grad, table = take(6)
    sums = take(count)
    total, chunk, low_tile, low, chunk_sems, output_sem, staged = take(7)
    images_now, seq, width = staged.shape
    now = pl.program_id(0)
    tile = low_tile.shape[1]
    slots = middle_slots()
    beside = Beside(now, slots)
    if count:
        at = place()
        copies = Copies(at, *take(2))
        chains = scatter_chains(copies, [(g, 0.0, g, None) for g in grads], sums, refs)
        beside = Beside(now, slots, issue_order(chains))

    def first_load():
        return pltpu.make_async_copy(middle, total, chunk_sems.at[images_now])

    def chunk_load(image):
        here = pl.ds(image * rows, rows)
        return pltpu.make_async_copy(middle.at[here], chunk, chunk_sems.at[image])

    def store():
        return pltpu.make_async_copy(staged, output, output_sem.at[0])

    @pl.when(now == 0)
    def _():
        first_load().start()
        if count:
            greet(at)
        table[...] = jnp.zeros(table.shape, F32)

    beside.at(0, MLP_STEPS, 0)

    @pl.when(now < MLP_STEPS)
    def _():
        pre = mm_nt(branch[...], down_tile[...]) * slope_tile[...].astype(F32)
        value = pre.astype(BF)
        low_tile[...] = value
        per_row = width // tile
        table[
            pl.ds(7 + now // per_row, 1), pl.ds(pl.multiple_of(now % per_row * tile, LANES), tile)
        ] = jnp.sum(value.astype(F32), axis=0, keepdims=True)

    beside.at(0, MLP_STEPS, 1)

    @pl.when(now < MLP_STEPS)
    def _():
        share = mm_nt(low_tile[...], up_tile[...])

        @pl.when(now == 0)
        def _():
            norm_in[...] = share

        @pl.when(now > 0)
        def _():
            norm_in[...] = norm_in[...] + share

    beside.at(0, MLP_STEPS, 2)

    @pl.when(now < MLP_STEPS)
    def _():
        up_grad[...] = mm_tn(n_two[...], low_tile[...]).astype(BF)

    beside.at(0, MLP_STEPS, 3)

    @pl.when(now < MLP_STEPS)
    def _():
        pl.when(now == 0)(lambda: first_load().wait())
        total[...] = total[...] + mm(act_tile[...], down_tile[...])

    @pl.when(now == MLP_STEPS)
    def _():
        chunk_load(0).start()
        for image in range(images_now):
            beside_image = image * rows
            staged[image] = (total[beside_image : beside_image + seq] + smalls[11:12]).astype(BF)
        store().start()

    for image in range(images_now):
        if image < 2:
            beside.at(MLP_STEPS, MLP_STEPS + 1, image)

        @pl.when(now == MLP_STEPS)
        def _(image=image):
            here = slice(image * rows, (image + 1) * rows)
            chunk_load(image).wait()
            normed, inverse = norm_stats(chunk[...])
            given = norm_in[here]
            out_grad = branch[here].astype(F32)
            result = out_grad + norm_back(normed, inverse, smalls[5:6], given)
            norm_in[here] = result
            value = result.astype(BF)
            low[here] = value
            for row, part in (
                (4, value.astype(F32)),
                (5, given * normed),
                (6, given),
                (11, out_grad),
            ):
                table[row : row + 1] = table[row : row + 1] + jnp.sum(part, axis=0, keepdims=True)
            if image + 1 < images_now:
                chunk_load(image + 1).start()

    beside.at(MLP_STEPS + 1, MLP_STEPS + 2, 0)

    @pl.when(now == MLP_STEPS + 1)
    def _():
        heads_grad[...] = mm_nt(low[...], proj[...]).astype(BF)

    beside.at(MLP_STEPS + 1, MLP_STEPS + 2, 1)

    @pl.when(now == MLP_STEPS + 1)
    def _():
        proj_grad[...] = mm_tn(heads[...], low[...]).astype(BF)
        store().wait()
        if count:
            copies.drain()


def middle_back(branch, act, slope, down, up, n_two, heads, proj, smalls, middle, out_shape, sums=()):
    tokens, width = branch.shape
    rows = tokens // out_shape[0]
    units = up.shape[1]
    tile = units // MLP_STEPS
    count = len(sums)
    shapes = block_shapes(sums)
    anywhere = pl.BlockSpec(memory_space=pl.ANY)

    def whole(shape):
        return pl.BlockSpec(shape, lambda s: (0,) * len(shape), pipeline_mode=pl.Buffered(1))

    def tile_at(s):
        return jnp.minimum(s, MLP_STEPS - 1)

    columns = pl.BlockSpec((tokens, tile), lambda s: (0, tile_at(s)))
    up_columns = pl.BlockSpec((width, tile), lambda s: (0, tile_at(s)))
    all_tokens = whole((tokens, width))
    params = dict(vmem_limit_bytes=VMEM_LIMIT)
    scratch = [
        pltpu.VMEM((tokens, width), F32),
        pltpu.VMEM((rows, width), F32),
        pltpu.VMEM((tokens, tile), BF),
        pltpu.VMEM((tokens, width), BF),
        pltpu.SemaphoreType.DMA((out_shape[0] + 1,)),
        pltpu.SemaphoreType.DMA((1,)),
        pltpu.VMEM(out_shape, BF),
    ]
    if count:
        params.update(collective_id=5, has_side_effects=True)
        scratch += scatter_scratch([(shape, True) for shape in shapes])
    return pl.pallas_call(
        functools.partial(middle_kernel, rows, count),
        grid=(MLP_STEPS + 2,),
        in_specs=[
            all_tokens,
            columns,
            columns,
            pl.BlockSpec((tile, width), lambda s: (tile_at(s), 0)),
            up_columns,
            all_tokens,
            all_tokens,
            whole((width, width)),
            whole((SMALL_ROWS, width)),
            anywhere,
        ]
        + [anywhere] * count,
        out_specs=[
            up_columns,
            anywhere,
            all_tokens,
            all_tokens,
            whole((width, width)),
            whole((SMALL_ROWS, width)),
        ]
        + [whole(shape) for shape in shapes],
        out_shape=[
            jax.ShapeDtypeStruct((width, units), BF),
            jax.ShapeDtypeStruct(out_shape, BF),
            jax.ShapeDtypeStruct((tokens, width), F32),
            jax.ShapeDtypeStruct((tokens, width), BF),
            jax.ShapeDtypeStruct((width, width), BF),
            jax.ShapeDtypeStruct((SMALL_ROWS, width), F32),
        ]
        + [jax.ShapeDtypeStruct(shape, F32) for shape in shapes],
        scratch_shapes=scratch,
        compiler_params=pltpu.CompilerParams(**params),
        cost_estimate=pl.CostEstimate(
            flops=2 * tokens * width * (4 * units + 2 * width),
            bytes_accessed=2 * (10 * tokens * width + 3 * width * units + 2 * tokens * units),
            transcendentals=0,
        ),
        name="middle_back",
    )(branch, act, slope, down, up, n_two, heads, proj, smalls, middle, *blocked(sums))


def last_slots(pairs_now):
    slots, step = [], 0
    for _ in range(TURNS):
        for _ in range(pairs_now // TURNS):
            slots += [(step, 0, 1.6), (step, 1, 1.6)]
            step += 1
        slots += [(step, 0, 2.2), (step, 1, 2.4), (step, 2, 0.1)]
        step += 1
    return slots + [(step, 0, 4.0), (step, 1, 0.0)]


def last_kernel(seq, rows, scale, count, *refs):
    refs = list(refs)

    def take(number):
        out = refs[:number]
        del refs[:number]
        return out

    q_ref, k_ref, v_ref, g_ref, log_ref, n_one = take(6)
    w_tiles = take(3)
    images, middle_grad, partial, smalls = take(4)
    grads = take(count)
    if count:
        (input_grad,) = take(1)
        sums = take(count + 1)
        small_outs = take(len(SMALL_AT))
    else:
        input_grad, tiles, table = take(3)
    g_part, norm_in, chunk, staged, chunk_sems, output_sem = take(6)
    if count:
        tiles, table = take(2)
    images_now, _, width = images.shape
    pairs = width // LANES
    pairs_now = images_now * pairs
    group_steps = pairs_now // TURNS
    period = group_steps + 1
    last = TURNS * period
    part_width = width // TURNS
    now = pl.program_id(0)
    group, inside = now // period, now % period
    slots = last_slots(pairs_now)
    beside = Beside(now, slots)
    if count:
        held, found, send_sems, recv_sems = take(4)
        at = place()
        copies = Copies(at, send_sems, recv_sems)
        earliest = {"small": (last, 1)}
        fulls = [(g, 0.0, number, None) for number, g in enumerate(grads)]
        for tile in range(TURNS):
            key = (tile * period + group_steps, 2)
            tag = ("tile", tile)
            earliest[tag] = key

            def column(begin, tile=tile):
                return begin // part_width * width + tile * part_width + begin % part_width

            fulls.append((tiles.at[tile], slot_start(slots, key), tag, column))
        chains = scatter_chains(copies, fulls, sums, refs)
        chains.append(
            (slot_start(slots, (last, 1)), "small", small_chain(copies, held, found, table))
        )
        beside = Beside(now, slots, issue_order(chains), 0.0, earliest)

    def chunk_load(image):
        here = pl.ds(image * rows, rows)
        return pltpu.make_async_copy(
            middle_grad.at[here], chunk.at[image % 2], chunk_sems.at[image % 2]
        )

    def store():
        return pltpu.make_async_copy(staged, input_grad, output_sem.at[0])

    if count:
        pl.when(now == 0)(lambda: greet(at))
    attending = (now < last) & (inside < group_steps)
    place_now = group * group_steps + inside
    for head in range(LANES // HD):
        for turn in range(TURNS):
            beside.at(turn * period, turn * period + group_steps, head)

        @pl.when(attending)
        def _(head=head):
            here = pl.ds(pl.multiple_of((place_now % images_now) * rows, 16), rows)
            pair = place_now // images_now % (pairs // TURNS)
            mask = head_masks((rows, LANES))[head]
            parts = attend_head_back(
                seq,
                scale,
                mask,
                q_ref[...],
                k_ref[...],
                v_ref[...],
                g_ref[...],
                log_ref[0, 0, head : head + 1, :],
            )
            for number, part in enumerate(parts):
                lanes = pl.ds(pl.multiple_of(number * part_width + pair * LANES, LANES), LANES)
                g_part[here, lanes] = part if head == 0 else g_part[here, lanes] + part

    for turn in range(TURNS):
        step = turn * period + group_steps
        beside.at(step, step + 1, 0)

        @pl.when(now == step)
        def _(turn=turn):
            value = mm_tn(n_one[...], g_part[...]).astype(BF)
            tiles[turn] = value.reshape(tiles.shape[1:])

        beside.at(step, step + 1, 1)

        @pl.when(now == step)
        def _(turn=turn):
            given = g_part[...]
            share = mm_nt(given, jnp.concatenate([w_tile[...] for w_tile in w_tiles], axis=1))
            if turn == 0:
                norm_in[...] = share
                table[...] = partial[...]
            else:
                norm_in[...] = norm_in[...] + share
            begin = turn * part_width
            for part in (0, 2):
                table[2 + part // 2 : 3 + part // 2, begin : begin + part_width] = jnp.sum(
                    given[:, part * part_width : (part + 1) * part_width].astype(F32),
                    axis=0,
                    keepdims=True,
                )

        beside.at(step, step + 1, 2)

    beside.at(last, last + 1, 0)

    @pl.when(now == last)
    def _():
        chunk_load(0).start()
        for image in range(images_now):
            chunk_load(image).wait()
            if image + 1 < images_now:
                chunk_load(image + 1).start()
            given = norm_in[image * rows : image * rows + seq]
            normed, inverse = norm_stats(images[image].astype(F32))
            more = norm_back(normed, inverse, smalls[0:1], given)
            staged[image] = (chunk[image % 2, 0:seq] + more).astype(BF)
            for row, part in ((0, given * normed), (1, given)):
                table[row : row + 1] = table[row : row + 1] + jnp.sum(part, axis=0, keepdims=True)
        store().start()
        if count:
            held[0] = table[...]

    beside.at(last, last + 1, 1)

    @pl.when(now == last)
    def _():
        if count:
            mine = (at["y"] * 2 + at["x"]) * 2 + at["core"]
            mine = mine * DEPTH + at["z"]
            for out, row in zip(small_outs, SMALL_AT):
                size = out.shape[1]
                whole = size * 8 * DEPTH
                spot = lax.broadcasted_iota(jnp.int32, (size, width), 0) + mine * size
                lane = lax.broadcasted_iota(jnp.int32, (size, width), 1)
                result = None
                for part in range(whole // width):
                    hot = jnp.where(lane + part * width == spot, 1.0, 0.0)
                    piece = lax.dot_general(
                        table[row + part : row + part + 1],
                        hot,
                        (((1,), (1,)), ((), ())),
                        precision=lax.Precision.HIGHEST,
                        preferred_element_type=F32,
                    )
                    result = piece if result is None else result + piece
                out[...] = result
            copies.drain()
        store().wait()


def last_back(parts, heads_grad, logs, n_one, joint, images, middle_grad, partial, smalls, small_in, rows, scale, sums=()):
    images_now, seq, width = images.shape
    tokens = images_now * rows
    pairs = width // LANES
    pairs_now = images_now * pairs
    group_steps = pairs_now // TURNS
    period = group_steps + 1
    part_width = width // TURNS
    heads = LANES // HD
    count = len(sums)
    shapes = block_shapes(sums)
    block = width // (8 * DEPTH)
    anywhere = pl.BlockSpec(memory_space=pl.ANY)

    def whole(shape):
        return pl.BlockSpec(shape, lambda s: (0,) * len(shape), pipeline_mode=pl.Buffered(1))

    def group_at(s):
        return jnp.minimum(s // period, TURNS - 1)

    def at(s):
        group = group_at(s)
        flat = group * group_steps + jnp.minimum(s - group * period, group_steps - 1)
        return flat % images_now, flat // images_now

    def columns(part):
        return pl.BlockSpec((width, part_width), lambda s: (0, part * TURNS + group_at(s)))

    own = pl.BlockSpec((rows, LANES), at)
    tiles_shape = (TURNS, 2, 2, 2, DEPTH, block, 3 * part_width)
    table_shape = (SMALL_ROWS, width)
    params = dict(vmem_limit_bytes=VMEM_LIMIT)
    scratch = [
        pltpu.VMEM((tokens, 3 * part_width), BF),
        pltpu.VMEM((tokens, width), F32),
        pltpu.VMEM((2, rows, width), F32),
        pltpu.VMEM(images.shape, BF),
        pltpu.SemaphoreType.DMA((2,)),
        pltpu.SemaphoreType.DMA((1,)),
    ]
    out_specs = [anywhere]
    out_shape = [jax.ShapeDtypeStruct(images.shape, BF)]
    if count:
        params.update(collective_id=2, has_side_effects=True)
        own_shapes = shapes + [(block, 3 * width)] + [(1, v.shape[0]) for v in small_in]
        out_specs += [whole(shape) for shape in own_shapes]
        out_shape += [jax.ShapeDtypeStruct(shape, F32) for shape in own_shapes]
        scratch += [pltpu.VMEM(tiles_shape, BF), pltpu.VMEM(table_shape, F32)] + small_scratch()
        kinds = [(shape, True) for shape in shapes]
        kinds += [((block, 3 * part_width), False)] * TURNS
        scratch += scatter_scratch(kinds, SMALL_COPIES)
    else:
        out_specs += [whole(tiles_shape), whole(table_shape)]
        out_shape += [
            jax.ShapeDtypeStruct(tiles_shape, BF),
            jax.ShapeDtypeStruct(table_shape, F32),
        ]
    return pl.pallas_call(
        functools.partial(last_kernel, seq, rows, scale, count),
        grid=(TURNS * period + 1,),
        in_specs=[
            own,
            own,
            own,
            own,
            pl.BlockSpec((1, 1, heads, rows), lambda s: at(s) + (0, 0)),
            whole((tokens, width)),
            columns(0),
            columns(1),
            columns(2),
            whole(images.shape),
            anywhere,
            whole(table_shape),
            whole(table_shape),
        ]
        + [anywhere] * count,
        out_specs=out_specs,
        out_shape=out_shape,
        scratch_shapes=scratch,
        compiler_params=pltpu.CompilerParams(**params),
        cost_estimate=pl.CostEstimate(
            flops=10 * images_now * HEADS * rows * rows * LANES * 2 + 12 * tokens * width * width,
            bytes_accessed=tokens * width * 24 + width * width * 12,
            transcendentals=images_now * HEADS * rows * rows,
        ),
        name="last_back",
    )(*parts, heads_grad, logs, n_one, joint, joint, joint, images, middle_grad, partial, smalls, *blocked(sums))


ORDERS = (("x", "z", "y"), ("y", "z", "x"), ("z", "x", "y"), ("z", "y", "x"))
SHARES = (4, 4, 8, 8)


def place():
    dev = lax.axis_index("dev")
    return dict(
        core=dev % 2, x=(dev // 2) % 2, y=dev // 4, z=lax.axis_index("rep")
    )


def peer(at, axis, step=0):
    other = dict(at)
    other[axis] = (at[axis] + step) % DEPTH if axis == "z" else 1 - at[axis]
    return {"dev": (other["y"] * 2 + other["x"]) * 2 + other["core"], "rep": other["z"]}


def greet(at):
    barrier = pltpu.get_barrier_semaphore()
    peers = [("core", 0), ("x", 0), ("y", 0)] + [("z", step) for step in range(1, DEPTH)]
    for axis, step in peers:
        pl.semaphore_signal(barrier, 1, device_id=peer(at, axis, step), device_id_type=MESH)
    pl.semaphore_wait(barrier, len(peers))


def cuts(columns):
    units = columns // 128
    total = sum(SHARES)
    out, at, seen = [], 0, 0
    for order, share in zip(ORDERS, SHARES):
        seen += share
        end = round(units * seen / total)
        if end > at:
            out.append((order, at * 128, (end - at) * 128))
        at = end
    return out


class Copy:
    def __init__(self, owner, number, source, target, axis, step):
        self.owner, self.number, self.source, self.target = owner, number, source, target
        self.axis, self.step = axis, step

    def build(self):
        return pltpu.make_async_remote_copy(
            src_ref=self.source(),
            dst_ref=self.target(),
            send_sem=self.owner.send_sems.at[self.number],
            recv_sem=self.owner.recv_sems.at[self.number],
            device_id=peer(self.owner.at, self.axis, self.step),
            device_id_type=MESH,
        )

    def start(self):
        self.build().start()

    def wait_send(self):
        self.build().wait_send()

    def wait_recv(self):
        self.build().wait_recv()


class Copies:
    def __init__(self, at, send_sems, recv_sems):
        self.at, self.send_sems, self.recv_sems = at, send_sems, recv_sems
        self.all = []

    def make(self, source, target, axis, step=0):
        copy = Copy(self, len(self.all), source, target, axis, step)
        self.all.append(copy)
        return copy

    def drain(self):
        for copy in self.all:
            copy.wait_send()


LINK = {"x": 90.0, "y": 90.0, "z": 90.0, "core": 500.0}
HOP_US = 2.0
LEAD_US = 1.0


def issue_order(chains):
    free = dict.fromkeys(LINK, 0.0)
    queue = [(chain[0], number, 0) for number, chain in enumerate(chains)]
    heapq.heapify(queue)
    out = []
    while queue:
        ready, number, step = heapq.heappop(queue)
        _, tag, steps = chains[number]
        links, size, run = steps[step]
        begin = max([ready] + [free[link] for link in links])
        done = begin
        for link in links:
            free[link] = begin + size / LINK[link]
            done = max(done, free[link] + HOP_US)
        out.append((max(ready, begin - LEAD_US), tag, run))
        if step + 1 < len(steps):
            heapq.heappush(queue, (done, number, step + 1))
    return sorted(out, key=lambda event: event[0])


def gather_chain(copies, shard, full, order, columns, own_ready):
    at = copies.at
    steps = []
    begin, width = columns
    size = 2 * full.shape[4] * width * 2 / 1000.0
    pending = []

    def region(held):
        def along(axis, extent):
            return pl.ds(0, extent) if axis in held else at[axis]

        y, x, z = along("y", 2), along("x", 2), along("z", DEPTH)
        return full.at[y, x, at["core"], z, :, pl.ds(begin, width)]

    def step(links, size, copies_now, own=False):
        before = list(pending)
        pending.clear()
        pending.extend(copies_now)

        def prepare():
            own_wait = own_ready() if own else None

            def run():
                if own_wait is not None:
                    own_wait()
                for copy in before:
                    copy.wait_recv()
                for copy in copies_now:
                    copy.start()

            return run

        steps.append((links, size, prepare))

    def first():
        return shard.at[:, pl.ds(begin, width)]

    held, blocks = (), 1
    for axis in order:
        here = functools.partial(region, held)
        if axis == "z":
            source = first if blocks == 1 else here
            now = [copies.make(source, here, "z", step_z) for step_z in range(1, DEPTH)]
            step(("z",), size * blocks * DEPTH, now, blocks > 1)
            blocks *= DEPTH
        else:
            copy = copies.make(first if blocks == 1 else here, here, axis)
            step((axis,), size * blocks, [copy], blocks > 1)
            blocks *= 2
        held += (axis,)
    whole = functools.partial(region, held)
    step(("core",), size * blocks / 2, [copies.make(whole, whole, "core")])
    step((), 0.0, [])
    return steps


def gathered_shapes(shards):
    return [jax.ShapeDtypeStruct((2, 2, 2, DEPTH) + s.shape, s.dtype) for s in shards]


def gather_chains(copies, shards, fulls, own_sems, releases):
    at = copies.at
    chains, owns = [], []
    for number, (shard, full, release) in enumerate(zip(shards, fulls, releases)):

        def own(number=number, shard=shard, full=full):
            mine = full.at[at["y"], at["x"], at["core"], at["z"]]
            return pltpu.make_async_copy(shard, mine, own_sems.at[number])

        owns.append(own)
        waited = []

        def ready(own=own, waited=waited):
            if waited:
                return None
            waited.append(True)
            return lambda: own().wait()

        if isinstance(release, tuple):
            parts = [(at_us, (number, g)) + cut for g, at_us in enumerate(release) for cut in group_cuts(g, full.shape[5] // 3)]
        else:
            parts = [(release, number) + cut for cut in cuts(full.shape[5])]
        for release_us, tag, order, begin, width in parts:
            steps = gather_chain(copies, shard, full, order, (begin, width), ready)
            chains.append((release_us, tag, steps))
    return owns, chains


def plain(run):
    return lambda: run


def in_turn(*events):
    def prepare():
        runs = [event() for event in events]

        def run():
            for one in runs:
                one()

        return run

    return prepare


def group_cuts(group, width):
    size = width // GROUPS
    begin = group * size
    return [
        (ORDERS[2], begin, size),
        (ORDERS[3], width + begin, size),
        (ORDERS[0], 2 * width + begin, size // 2),
        (ORDERS[1], 2 * width + begin + size // 2, size // 2),
    ]


SMALL_ROWS = 16
SMALL_COPIES = DEPTH + 2


def small_scratch():
    return [
        pltpu.VMEM((5, SMALL_ROWS, 1024), F32),
        pltpu.VMEM((SMALL_COPIES, SMALL_ROWS, 1024), F32),
    ]


def small_chain(copies, held, found, result):
    size = 2 * SMALL_ROWS * 1024 * 4 / 1000.0
    steps = []
    before = None
    used = 0
    for number, axis in enumerate(("core", "x", "y", "z")):
        now = []
        for step in range(1, DEPTH if axis == "z" else 2):
            source, landing = (
                functools.partial(lambda n: held.at[n], number),
                functools.partial(lambda n: found.at[n], used),
            )
            now.append((copies.make(source, landing, axis, step), used))
            used += 1

        def run(now=now, before=before):
            if before is not None:
                before()
            for copy, _ in now:
                copy.start()

        steps.append(((axis,), size * len(now), plain(run)))

        def before(now=now, number=number):
            total = held[number]
            for copy, slot in now:
                copy.wait_recv()
                total = total + found[slot]
            held[number + 1] = total

    def finish():
        before()
        result[...] = held[4]

    steps.append(((), 0.0, plain(finish)))
    return steps


def tile_cuts(columns):
    size = columns // 3
    return [
        (ORDERS[2], 0, size),
        (ORDERS[3], size, size),
        (ORDERS[0], 2 * size, size // 2),
        (ORDERS[1], 2 * size + size // 2, size // 2),
    ]


def chains_of(kinds):
    out = []
    for number, ((_, columns), staged) in enumerate(kinds):
        parts = cuts(columns) if staged else tile_cuts(columns)
        out.extend((number, order[::-1], begin, width) for order, begin, width in parts)
    return out


def scatter_buffers(order, rows, width):
    extents = {"y": 2, "x": 2, "z": DEPTH}
    block = (rows, width)
    shapes = [(2, 2, DEPTH) + block]
    held = []
    for axis in order:
        left = tuple(extents[a] for a in ("y", "x", "z") if a not in held and a != axis)
        shapes.append(((DEPTH - 1,) if axis == "z" else ()) + left + block)
        held.append(axis)
    return [pltpu.VMEM(shape, BF) for shape in shapes]


def scatter_scratch(kinds, more=0):
    chains = chains_of(kinds)
    copies = 6 * len(chains) + more
    widths = [c[3] for c in chains if kinds[c[0]][1]]
    rows = kinds[0][0][0]
    scratch = [
        pltpu.SemaphoreType.DMA((copies,)),
        pltpu.SemaphoreType.DMA((copies,)),
        pltpu.SemaphoreType.DMA((2,)),
        pltpu.VMEM((2, 2, 2, DEPTH, rows, max(widths)), BF),
    ]
    for number, order, _, width in chains:
        scratch += scatter_buffers(order, kinds[number][0][0], width)
    return scratch


class Stage:
    def __init__(self, sems, ref):
        self.sems, self.ref = sems, ref
        self.free, self.queue, self.held = list(range(ref.shape[0])), [], {}

    def view(self, slot, width):
        return self.ref.at[slot, :, :, :, :, pl.ds(0, width)]

    def build(self, slot, source, width):
        return pltpu.make_async_copy(source(), self.view(slot, width), self.sems.at[slot])

    def request(self, key, source, width):
        self.queue.append((key, source, width))
        return self.pump()

    def pump(self):
        starts = []
        while self.free and self.queue:
            key, source, width = self.queue.pop(0)
            self.held[key] = (self.free.pop(0), source, width)
            starts.append(functools.partial(self.begin, *self.held[key]))
        return starts

    def begin(self, slot, source, width):
        self.build(slot, source, width).start()

    def take(self, key):
        held = self.held[key]
        return lambda: self.build(*held).wait(), lambda: self.view(held[0], held[2])

    def give(self, key):
        self.free.append(self.held.pop(key)[0])
        return self.pump()


def add_blocks(target, source, extents):
    total = math.prod(extents)

    def one(flat, carry):
        index = []
        for extent in reversed(extents):
            index.insert(0, flat % extent)
            flat = flat // extent
        into, index = target(*index), tuple(index)
        into[...] = into[...] + source[index]
        return carry

    if total == 1:
        one(0, 0)
    else:
        lax.fori_loop(0, total, one, 0)


def scatter_chain(copies, full, out, out_begin, order, columns, buffers, stage):
    at = copies.at
    begin, width = columns
    total = buffers[0]
    size = 2 * full.shape[4] * width * jnp.dtype(full.dtype).itemsize / 1000.0
    extents = {"y": 2, "x": 2, "z": DEPTH}
    steps = []

    def half(core):
        return full.at[:, :, core, :, :, pl.ds(begin, width)]

    def region(held, **places):
        index = []
        for axis in ("y", "x", "z"):
            if axis in places:
                index.append(places[axis])
            else:
                index.append(at[axis] if axis in held else pl.ds(0, extents[axis]))
        return total.at[tuple(index)]

    def step(links, amount, run):
        steps.append((links, amount, run))

    core_copy = copies.make(lambda: half(1 - at["core"]), lambda: total, "core")
    key = id(core_copy)

    def begin_core():
        loads = [] if stage is None else stage.request(key, lambda: half(at["core"]), width)

        def run():
            core_copy.start()
            for load in loads:
                load()

        return run

    step(("core",), size * 8, begin_core)

    def add_core():
        own_wait, own, loads = None, lambda: half(at["core"]), ()
        if stage is not None:
            own_wait, own = stage.take(key)
            loads = stage.give(key)

        def run():
            core_copy.wait_recv()
            if own_wait is not None:
                own_wait()
            add_blocks(lambda y, x, z: total.at[y, x, z], own(), (2, 2, DEPTH))
            for load in loads:
                load()

        return run

    before = add_core
    held = ()
    blocks = 4 * DEPTH
    for axis, buffer in zip(order, buffers[1:]):
        left = [a for a in ("y", "x", "z") if a not in held and a != axis]
        counts = tuple(extents[a] for a in left)

        def block_at(held, axis, here, left, index):
            places = dict(zip(left, index))
            return region(held, **{axis: here}, **places)

        if axis == "z":
            blocks //= DEPTH
            now = []
            for step_z in range(1, DEPTH):

                def source(held=held, step_z=step_z):
                    return region(held, z=(at["z"] + step_z) % DEPTH)

                def landing(buffer=buffer, step_z=step_z):
                    return buffer.at[step_z - 1]

                now.append((copies.make(source, landing, "z", step_z), landing))

            def starts(now=now):
                for copy, _ in now:
                    copy.start()

            step(("z",), size * blocks * DEPTH, in_turn(before, plain(starts)))

            def arrive(now=now, held=held, left=left, counts=counts):
                for copy, landing in now:
                    copy.wait_recv()
                    add_blocks(
                        lambda *index: block_at(held, "z", at["z"], left, index), landing(), counts
                    )

            before = plain(arrive)

        else:
            blocks //= 2
            copy = copies.make(
                lambda held=held, axis=axis: region(held, **{axis: 1 - at[axis]}),
                lambda buffer=buffer: buffer,
                axis,
            )

            step((axis,), size * blocks, in_turn(before, plain(copy.start)))

            def arrive(copy=copy, buffer=buffer, held=held, axis=axis, left=left, counts=counts):
                copy.wait_recv()
                add_blocks(
                    lambda *index: block_at(held, axis, at[axis], left, index), buffer, counts
                )

            before = plain(arrive)

        held += (axis,)

    def finish():
        out[:, out_begin : out_begin + width] = total[at["y"], at["x"], at["z"]].astype(F32)

    step((), 0.0, in_turn(before, plain(finish)))
    return steps


def scatter_chains(copies, fulls, outs, scratch):
    kinds = [(full.shape[4:], column is None) for full, _, _, column in fulls]
    stage_sems, stage_ref = scratch[:2]
    stage = Stage(stage_sems, stage_ref)
    buffers = scratch[2:]
    chains = []
    for number, order, begin, width in chains_of(kinds):
        full, release, tag, column = fulls[number]
        mine, buffers = buffers[:4], buffers[4:]
        out = outs[number] if column is None else outs[-1]
        steps = scatter_chain(
            copies,
            full,
            out,
            begin if column is None else column(begin),
            order,
            (begin, width),
            mine,
            stage if column is None else None,
        )
        chains.append((release, tag, steps))
    return chains


def block_shapes(grads):
    return [(g.shape[0] // (8 * DEPTH), g.shape[1]) for g in grads]


def blocked(grads):
    return [
        g.reshape((2, 2, 2, DEPTH) + shape) for g, shape in zip(grads, block_shapes(grads))
    ]


def index_bits(sizes):
    dev, rep = sizes
    out = []
    for size, stride, axis in ((dev, rep, "dev"), (rep, 1, "rep")):
        for bit in reversed(range(size.bit_length() - 1)):
            step = stride << bit
            out.append((axis, bit, [(i, i ^ step) for i in range(dev * rep)]))
    return out


def scatter_sum(full, sizes, orders):
    bits = index_bits(sizes)
    count = sizes[0] * sizes[1]
    rows = full.shape[0] // count
    pieces = []
    cut = full.shape[1] // len(orders)
    for number, order in enumerate(orders):
        value = full[:, number * cut : (number + 1) * cut]
        value = value.reshape((2,) * len(bits) + (rows, cut))
        left = list(range(len(bits)))
        for which in order:
            axis, bit, flips = bits[which]
            place = left.index(which)
            mine = (lax.axis_index(axis) >> bit) & 1
            send = lax.dynamic_index_in_dim(value, 1 - mine, place, keepdims=False)
            keep = lax.dynamic_index_in_dim(value, mine, place, keepdims=False)
            value = keep + lax.ppermute(send, AXES, flips)
            left.remove(which)
        pieces.append(value.reshape(rows, cut))
    return jnp.concatenate(pieces, axis=1).astype(F32)


def norm_stats(values):
    centred = values - jnp.mean(values, axis=-1, keepdims=True)
    spread = jnp.mean(centred * centred, axis=-1, keepdims=True)
    inverse = lax.rsqrt(spread + EPS)
    return centred * inverse, inverse


def norm_back(normed, inverse, gain, grad):
    scaled = grad * gain
    return inverse * (
        scaled
        - jnp.mean(scaled, axis=-1, keepdims=True)
        - normed * jnp.mean(scaled * normed, axis=-1, keepdims=True)
    )


def gelu_and_slope(values):
    half = 0.5 * (1.0 + lax.erf(values * (1.0 / math.sqrt(2.0))))
    bell = jnp.exp(-0.5 * values * values) * (1.0 / math.sqrt(2.0 * math.pi))
    return values * half, half + values * bell


def body(sizes, *args):
    images, cotangent, filled = args[0], args[13], args[14]
    small_in = (args[1], args[2], args[4], args[6], args[7], args[8], args[10], args[12])
    big_in = (args[3], args[5], args[9], args[11])
    count = sizes[0] * sizes[1]
    images_now, seq, width = images.shape
    rows = -(-seq // 16) * 16
    tokens = images_now * rows
    scale = 1.0 / math.sqrt(HD)

    fast = sizes == FAST_MESH
    if fast:
        smalls, weights = small_in, big_in
    else:
        packed = lax.all_gather(jnp.concatenate(small_in)[None], AXES, axis=0, tiled=True)
        pieces, at = [], 0
        for one in small_in:
            pieces.append(packed[:, at : at + one.shape[0]].reshape(-1, width).astype(F32))
            at += one.shape[0]
        smalls = jnp.concatenate(pieces)
        smalls = jnp.pad(smalls, ((0, SMALL_ROWS - smalls.shape[0]), (0, 0)))
        weights = [lax.all_gather(w, AXES, axis=0, tiled=True) for w in big_in]
    queries, keys, values, logs, branch, heads_out, normed_one, middle, normed_two, *more = forward(
        images, cotangent, filled, rows, seq, scale, smalls, weights
    )
    activated, slope, down_grad, *found = more
    if fast:
        smalls, *weights = found
        weights = [w.reshape(count * shard.shape[0], -1) for w, shard in zip(weights, big_in)]
    joint_w, proj_w, up_w, down_w = weights
    up_grad, output, middle_grad, heads_grad, proj_grad, partial, *down_sum = middle_back(
        branch,
        activated,
        slope,
        down_w,
        up_w,
        normed_two,
        heads_out,
        proj_w,
        smalls,
        middle,
        images.shape,
        (down_grad,) if fast else (),
    )
    input_grad, *found = last_back(
        (queries, keys, values),
        heads_grad,
        logs,
        normed_one,
        joint_w,
        images,
        middle_grad,
        partial,
        smalls,
        small_in,
        rows,
        scale,
        (up_grad, proj_grad) if fast else (),
    )
    if fast:
        (down_sum,), (up_sum, proj_sum, joint_sum), shares = down_sum, found[:3], found[3:]
        shares = [share[0] for share in shares]
    else:
        tiles, table = found
        tiles = tiles.reshape(TURNS, width, 3, -1)
        joint_grad = tiles.transpose(1, 2, 0, 3).reshape(width, -1)
        orders = scatter_orders(sizes)
        down_sum, up_sum, proj_sum, joint_sum = [
            scatter_sum(g, sizes, orders) for g in (down_grad, up_grad, proj_grad, joint_grad)
        ]
        ends = SMALL_AT[1:] + (SMALL_AT[-1] + 1,)
        stacked = jnp.concatenate(
            [table[row:end].reshape(count, -1) for row, end in zip(SMALL_AT, ends)], axis=1
        )
        mine = lax.psum_scatter(stacked, AXES, scatter_dimension=0, tiled=True).reshape(-1)
        shares, at = [], 0
        for one in small_in:
            shares.append(mine[at : at + one.shape[0]])
            at += one.shape[0]
    return (
        output,
        input_grad,
        shares[0],
        shares[1],
        joint_sum,
        shares[2],
        proj_sum,
        shares[3],
        shares[4],
        shares[5],
        up_sum,
        shares[6],
        down_sum,
        shares[7],
    )


def scatter_orders(sizes):
    bits = len(index_bits(sizes))
    devs = sizes[0].bit_length() - 1
    reps = list(range(devs, bits))
    if devs < 3:
        return [list(range(bits))] * 2
    inner = list(range(devs - 3))
    y, x, core = devs - 3, devs - 2, devs - 1
    return [[core, x, y] + inner + reps, [core, y, x] + inner + reps]


def solution(mesh):
    sizes = (mesh.shape["dev"], mesh.shape["rep"])
    both = ("dev", "rep")
    three, one, two = P(both, None, None), P(both), P(both, None)
    in_specs = (three, one, one, two, one, two, one, one, one, two, one, two, one, three, one)
    out_specs = (three, three, one, one, two, one, two, one, one, one, two, one, two, one)
    return jax.shard_map(
        functools.partial(body, sizes),
        mesh=mesh,
        in_specs=in_specs,
        out_specs=out_specs,
        check_vma=False,
    )
```
